128 devices in a mesh: band: 8 (over z, core), chan: 16 (over x, y).
Axes of the slice: x: 4, y: 4, z: 4, core: 2. Of those that a mesh axis runs over, the one named last changes fastest.
Arguments:
- voltages: bfloat16 [128, 2, 512, 2048], P('band', None, None, 'chan'), may hold values from -6 to 6
- weights: bfloat16 [128, 2, 2048, 2048], P(('band', 'chan')), may hold values from -0.125 to 0.125
- beam_order: int32 [2048], replicated, may hold values from 0 to 2047, each once
- delay_merge_tables: int32 [127, 64, 3], replicated, may hold values from 0 to 63, as said below
Outputs:
- fdmt_out: float32 [2048, 64, 128], P(('band', 'chan'))
The draws below stay inside these ranges and needn't reach their ends.
Inputs may be any that keep to these rules, and one draw needn't show every extreme that they name: `beam_order`: each beam appears exactly once. `delay_merge_tables`: row 128 - (128 >> (l - 1)) + g is the node of level l (l = 1, ..., log2 128) that merges groups 2 g and 2 g + 1 of 2**(l - 1) adjacent channels each; for delays d < min(64, 2**(l + 1)) column 0 and column 1 are delays of the lower and the upper group, below the lower level's delay count (1 at level 1, else min(64, 2**l)), and column 2 is the time shift of the upper group, below min(64, 2**(l + 1)); the shifts of the used delays of one node are distinct; entries of larger delays are not read.
All inputs are finite; a program needn't handle non-finite values.
Results may differ from the reference program's by a relative error of at most 0.0003.
Values may be sent and summed in bfloat16 or wider, within the bound.
A program may use at most 128 MiB of HBM per device.

```python
import functools
import math
import jax
import jax.numpy as jnp
from jax import lax

ANTENNA_COUNT = 2048
FORMED_BEAMS = 2048
DELAYS = 64
TIME_SAMPLES = 512
TAVG = 128
FREQ_CHANNELS = 128


def draw_delay_merge_tables(key, part):
    levels = FREQ_CHANNELS.bit_length() - 1
    pieces = []
    for level_index in range(1, levels + 1):
        groups = FREQ_CHANNELS >> level_index
        delay_count = min(DELAYS, 2 ** (level_index + 1))
        before = 1 if level_index == 1 else min(DELAYS, 2 ** level_index)
        level_key = jax.random.fold_in(key, 7919 + level_index)
        key_low, key_high, key_shift, key_rest = jax.random.split(level_key, 4)
        low_part = jax.random.randint(key_low, (groups, DELAYS), 0, before, dtype=jnp.int32)
        high_part = jax.random.randint(key_high, (groups, DELAYS), 0, before, dtype=jnp.int32)
        shift_keys = jax.random.split(key_shift, groups)
        shift_used = jax.vmap(lambda one_key: jax.random.permutation(one_key, delay_count))(shift_keys).astype(jnp.int32)
        shift_rest = jax.random.randint(key_rest, (groups, DELAYS - delay_count), 0, delay_count, dtype=jnp.int32)
        shift_part = jnp.concatenate([shift_used, shift_rest], axis=1)
        pieces.append(jnp.stack([low_part, high_part, shift_part], axis=-1))
    return jnp.concatenate(pieces, axis=0)


def block_scale(key, shape, shards, smallest, top_value):
    def one(position, parts):
        steps = jax.random.uniform(jax.random.fold_in(jax.random.fold_in(key, 6), position), (parts,), jnp.float32, smallest / len(shards), top_value / len(shards))
        return jnp.repeat(jnp.exp(steps), shape[position] // parts).reshape((-1,) + (1,) * (len(shape) - position - 1))

    level = one(*shards[0])
    for cut in shards[1:]:
        level = level * one(*cut)
    return level


def gaussian(rng, extent, deviation, reach, cuts=(), kind=jnp.bfloat16):
    array = jax.random.normal(rng, extent, jnp.float32) * deviation
    if len(cuts) > 0:
        array = block_scale(rng, extent, cuts, -0.22, 0.18) * array
    return jnp.clip(array, min=-reach, max=reach).astype(kind)


def setup_inputs(seed: int = 0) -> dict:
    key_list = jax.random.split(jax.random.key(seed), 5)
    return {
        "voltages": gaussian(key_list[0], (FREQ_CHANNELS, 2, TIME_SAMPLES, ANTENNA_COUNT), 1.0, 6.0, ((0, 8), (3, 16))),
        "weights": gaussian(key_list[1], (FREQ_CHANNELS, 2, ANTENNA_COUNT, FORMED_BEAMS), ANTENNA_COUNT ** -0.5, 0.125, ((0, 128),)),
        "beam_order": jax.random.permutation(key_list[2], FORMED_BEAMS).astype(jnp.int32),
        "delay_merge_tables": draw_delay_merge_tables(jax.random.fold_in(key_list[4], 71), 0),
    }


def merge_pair(lower_part, upper_part, table_rows, delay_count):
    in_use = table_rows[:delay_count]
    taken_low = jnp.take(lower_part, in_use[:, 0], axis=-2)
    taken_high = jnp.take(upper_part, in_use[:, 1], axis=-2)
    time_len = taken_high.shape[-1]
    shifted_index = jnp.arange(time_len, dtype=jnp.int32)[None, :] + in_use[:, 2][:, None]
    inside = shifted_index < time_len
    clipped = jnp.minimum(shifted_index, time_len - 1)
    picked = jnp.take_along_axis(taken_high, jnp.broadcast_to(clipped, taken_high.shape), axis=-1)
    return taken_low + jnp.where(inside, picked, 0.0)

def normalize(power_avg):
    time_mean = lax.optimization_barrier(jnp.mean(power_avg, axis=-1, keepdims=True))
    centered = power_avg - time_mean
    spread = lax.optimization_barrier(jnp.mean(centered * centered, axis=-1, keepdims=True))
    return centered / jnp.sqrt(spread + 1e-05)

def beam_power(inputs):
    voltage_channel, weight_chan = inputs
    stacked_beams = voltage_channel.reshape(2 * TIME_SAMPLES, ANTENNA_COUNT)
    first_sum = jnp.dot(stacked_beams, weight_chan[0], preferred_element_type=jnp.float32)
    second = jnp.dot(stacked_beams, weight_chan[1], preferred_element_type=jnp.float32)
    real_part = first_sum[:TIME_SAMPLES] - second[TIME_SAMPLES:]
    imag_part = second[:TIME_SAMPLES] + first_sum[TIME_SAMPLES:]
    power_all = (real_part * real_part + imag_part * imag_part).reshape(TAVG, 4, FORMED_BEAMS)
    return lax.optimization_barrier(jnp.mean(power_all, axis=1)).T

def reference(voltages, weights, beam_order, delay_merge_tables):
    powers = lax.map(beam_power, (voltages, weights))
    ordered = powers[:, beam_order]
    normed = normalize(ordered)
    transform_state = normed[:, :, None, :]
    levels = FREQ_CHANNELS.bit_length() - 1
    for level_index in range(1, levels + 1):
        groups = FREQ_CHANNELS >> level_index
        first_row = FREQ_CHANNELS - (FREQ_CHANNELS >> level_index - 1)
        table_part = delay_merge_tables[first_row:first_row + groups]
        delay_count = min(DELAYS, 2 ** (level_index + 1))
        merger = functools.partial(merge_pair, delay_count=delay_count)
        transform_state = jax.vmap(merger)(transform_state[0::2], transform_state[1::2], table_part)
    return transform_state[0] * (1.0 / math.sqrt(FREQ_CHANNELS))
```

```python
import functools
import math

import jax
import jax.numpy as jnp
from jax import lax
from jax.experimental import pallas as pl
from jax.experimental.pallas import tpu as pltpu
from jax.sharding import PartitionSpec as P

MESH = pl.DeviceIdType.MESH
DELAYS = 64
SIDE = 4
CHANS = 16
BANDS = 8
CHANNELS = CHANS * BANDS
BLOCK = 16
AVG = 128
SAMPLES = 512
TILE = 256

STEPS = (
    (0, 0), (0, 2), (3, 0), (1, 2), (3, 3), (1, 1), (3, 1), (0, 3),
    (1, 3), (2, 1), (2, 3), (3, 2), (1, 0), (2, 2), (0, 1), (2, 0),
)


def beam_kernel(v_ref, w_ref, order_hbm, out_ref, xbuf, wbuf, nbuf, acc, pw, norm, send, order,
                x_send, x_recv, w_sem, o_sem, ready, s_sem, r_sem):
    band = lax.axis_index("band")
    chan = lax.axis_index("chan")
    x, y = chan // SIDE, lax.rem(chan, SIDE)
    beams = w_ref.shape[3]
    tiles = beams // TILE

    def ahead(step):
        return lax.rem(x + step[0], SIDE) * SIDE + lax.rem(y + step[1], SIDE)

    def behind(step):
        return lax.rem(x + SIDE - step[0], SIDE) * SIDE + lax.rem(y + SIDE - step[1], SIDE)

    barrier = pltpu.get_barrier_semaphore()
    for step in STEPS[1:]:
        pl.semaphore_signal(barrier, inc=1, device_id={"band": band, "chan": ahead(step)}, device_id_type=MESH)
    for k in range(1, BANDS):
        pl.semaphore_signal(barrier, inc=1, device_id={"band": lax.rem(band + k, BANDS), "chan": chan}, device_id_type=MESH)

    own = pltpu.make_async_copy(v_ref.at[chan], xbuf.at[0], x_recv.at[0])
    own.start()
    loads = []
    for k, step in enumerate(STEPS):
        rows = pl.ds(pl.multiple_of(behind(step) * 128, 128), 128)
        for part in range(2):
            load = pltpu.make_async_copy(w_ref.at[0, part, rows, :], wbuf.at[k, pl.ds(part * 128, 128), :], w_sem.at[k])
            load.start()
            loads.append(load)
    order_copy = pltpu.make_async_copy(order_hbm, order, o_sem)
    order_copy.start()

    pl.semaphore_wait(barrier, CHANS - 1 + BANDS - 1)
    copies = []
    for k, step in enumerate(STEPS):
        if k == 0:
            continue
        peer = ahead(step)
        copy = pltpu.make_async_remote_copy(
            v_ref.at[peer], xbuf.at[k], x_send.at[k], x_recv.at[k],
            device_id={"band": band, "chan": peer}, device_id_type=MESH)
        copy.start()
        copies.append(copy)
    for step in STEPS[1:]:
        pl.semaphore_signal(ready, inc=1, device_id={"band": band, "chan": ahead(step)}, device_id_type=MESH)

    def arrived(k, slot):
        pltpu.make_async_copy(xbuf.at[k], xbuf.at[k], x_recv.at[k]).wait()
        pltpu.make_async_copy(wbuf.at[k], wbuf.at[k], w_sem.at[k]).wait()
        nbuf[slot] = -xbuf[k, 1]

    def lhs_of(ks):
        top, low = [], []
        for slot, k in enumerate(ks):
            top += [xbuf[k, 0], nbuf[slot]]
            low += [xbuf[k, 1], xbuf[k, 0]]
        return jnp.concatenate([jnp.concatenate(top, axis=1), jnp.concatenate(low, axis=1)], axis=0)

    def columns(n):
        return pl.ds(pl.multiple_of(n * TILE, TILE), TILE)

    def pair(j, first):
        k = 2 * j
        arrived(k, 0)
        arrived(k + 1, 1)

        def one_tile(n, carry):
            rhs = wbuf[pl.ds(k, 2), :, columns(n)].reshape(512, TILE)
            got = jnp.dot(lhs_of((k, k + 1)), rhs, preferred_element_type=jnp.float32)
            if first:
                acc[n] = got
            else:
                acc[n] += got
            return carry

        lax.fori_loop(0, tiles, one_tile, 0)

    pair(0, True)

    def later(j, carry):
        pair(j, False)
        return carry

    lax.fori_loop(1, 7, later, 0)
    arrived(14, 0)

    def single(n, carry):
        acc[n] += jnp.dot(lhs_of((14,)), wbuf[14, :, columns(n)], preferred_element_type=jnp.float32)
        return carry

    lax.fori_loop(0, tiles, single, 0)
    arrived(15, 0)

    def final(n, carry):
        got = acc[n] + jnp.dot(lhs_of((15,)), wbuf[15, :, columns(n)], preferred_element_type=jnp.float32)
        real, imag = got[:SAMPLES], got[SAMPLES:]
        power = real * real + imag * imag
        for half in range(TILE // 128):
            pw[half] = power[:, half * 128 : (half + 1) * 128]
            total = pw[half, pl.ds(0, AVG, stride=4), :]
            for t in range(1, 4):
                total = total + pw[half, pl.ds(t, AVG, stride=4), :]
            mean4 = total * 0.25
            centered = mean4 - jnp.mean(mean4, axis=0, keepdims=True)
            spread = jnp.mean(centered * centered, axis=0, keepdims=True)
            scaled = centered * (1.0 / jnp.sqrt(spread + 1e-05))
            norm[pl.ds(pl.multiple_of(n * TILE + half * 128, 128), 128), :] = scaled.T
        return carry

    lax.fori_loop(0, tiles, final, 0)
    for copy in copies:
        copy.wait_send()

    order_copy.wait()
    pl.semaphore_wait(ready, CHANS - 1)
    me = band * CHANS + chan

    def gather(r, block):
        for i in range(BLOCK):
            send[r, pl.ds(i, 1), :] = norm[pl.ds(order[block * BLOCK + i], 1), :]

    def one_send(r, carry):
        to_band = lax.rem(band + r // CHANS, BANDS)
        rc = lax.rem(r, CHANS)
        to_chan = lax.rem(x + rc // SIDE, SIDE) * SIDE + lax.rem(y + rc, SIDE)
        gather(r, to_band * CHANS + to_chan)
        pltpu.make_async_remote_copy(
            send.at[r], out_ref.at[me], s_sem, r_sem,
            device_id={"band": to_band, "chan": to_chan}, device_id_type=MESH).start()
        return carry

    lax.fori_loop(1, CHANNELS, one_send, 0)
    gather(0, me)
    keep = pltpu.make_async_copy(send.at[0], out_ref.at[me], o_sem)
    keep.start()
    keep.wait()
    others = pl.ds(1, CHANNELS - 1)
    pltpu.make_async_copy(send.at[others], send.at[others], s_sem).wait()
    pltpu.make_async_copy(send.at[others], send.at[others], r_sem).wait()


def beamform(voltages, weights, beam_order):
    beams = weights.shape[3]
    any_space = pl.BlockSpec(memory_space=pl.ANY)
    return pl.pallas_call(
        beam_kernel,
        out_shape=jax.ShapeDtypeStruct((CHANNELS, BLOCK, AVG), jnp.float32),
        in_specs=[any_space] * 3,
        out_specs=pl.BlockSpec(memory_space=pltpu.VMEM),
        scratch_shapes=[
            pltpu.VMEM((CHANS, 2, SAMPLES, 128), jnp.bfloat16),
            pltpu.VMEM((CHANS, 256, beams), jnp.bfloat16),
            pltpu.VMEM((2, SAMPLES, 128), jnp.bfloat16),
            pltpu.VMEM((beams // TILE, 2 * SAMPLES, TILE), jnp.float32),
            pltpu.VMEM((TILE // 128, SAMPLES, 128), jnp.float32),
            pltpu.VMEM((beams, AVG), jnp.float32),
            pltpu.VMEM((CHANNELS, BLOCK, AVG), jnp.float32),
            pltpu.SMEM((beams,), jnp.int32),
            pltpu.SemaphoreType.DMA((CHANS,)),
            pltpu.SemaphoreType.DMA((CHANS,)),
            pltpu.SemaphoreType.DMA((CHANS,)),
            pltpu.SemaphoreType.DMA,
            pltpu.SemaphoreType.REGULAR,
            pltpu.SemaphoreType.DMA,
            pltpu.SemaphoreType.DMA,
        ],
        compiler_params=pltpu.CompilerParams(
            collective_id=0, has_side_effects=True, vmem_limit_bytes=56 * 2**20),
    )(voltages, weights, beam_order)


def merge_kernel(table, start, out_ref, even, odd):
    lanes = lax.broadcasted_iota(jnp.int32, (BLOCK, AVG), 1)
    levels = CHANNELS.bit_length() - 1
    source, before = start, 1
    for level in range(1, levels + 1):
        groups = CHANNELS >> level
        count = min(DELAYS, 2 ** (level + 1))
        first_row = CHANNELS - (CHANNELS >> (level - 1))
        target = out_ref if level == levels else (even if level % 2 == 0 else odd)
        unroll = min(count, 8)
        parts = count // unroll

        def step(i, carry, source=source, target=target, before=before, count=count, first_row=first_row,
                 unroll=unroll, parts=parts, level=level):
            g = i // parts
            d0 = lax.rem(i, parts) * unroll
            for u in range(unroll):
                d = d0 + u
                r = first_row + g
                shift = table[2, d, r]
                low_row, high_row = 2 * g * before, (2 * g + 1) * before
                if level > 1:
                    low_row = low_row + table[0, d, r]
                    high_row = high_row + table[1, d, r]
                moved = pltpu.roll(source[high_row], lax.rem(AVG - shift, AVG), 1)
                merged = source[low_row] + jnp.where(lanes < AVG - shift, moved, 0.0)
                if level == levels:
                    target[:, pl.ds(d, 1), :] = (merged * (1.0 / math.sqrt(CHANNELS))).reshape(BLOCK, 1, AVG)
                else:
                    target[g * count + d] = merged
            return carry

        lax.fori_loop(0, groups * parts, step, 0)
        source, before = target, count


def dedisperse(start, tables):
    return pl.pallas_call(
        merge_kernel,
        out_shape=jax.ShapeDtypeStruct((BLOCK, DELAYS, AVG), jnp.float32),
        in_specs=[pl.BlockSpec(memory_space=pltpu.SMEM), pl.BlockSpec(memory_space=pltpu.VMEM)],
        out_specs=pl.BlockSpec(memory_space=pltpu.VMEM),
        scratch_shapes=[
            pltpu.VMEM((256, BLOCK, AVG), jnp.float32),
            pltpu.VMEM((256, BLOCK, AVG), jnp.float32),
        ],
        compiler_params=pltpu.CompilerParams(vmem_limit_bytes=32 * 2**20),
    )(jnp.transpose(tables, (2, 1, 0)), start)


def body(voltages, weights, beam_order, delay_merge_tables):
    regrouped = beamform(voltages, weights, beam_order)
    return dedisperse(regrouped, delay_merge_tables)


def solution(mesh):
    return jax.shard_map(
        body,
        mesh=mesh,
        in_specs=(P("band", None, None, "chan"), P(("band", "chan"), None, None, None), P(), P()),
        out_specs=P(("band", "chan"), None, None),
        check_vma=False,
    )
```

```python
import functools
import math

import jax
import jax.numpy as jnp
from jax import lax
from jax.experimental import pallas as pl
from jax.experimental.pallas import tpu as pltpu
from jax.sharding import PartitionSpec as P

MESH = pl.DeviceIdType.MESH
DELAYS = 64
SIDE = 4
CHANS = 16
BANDS = 8
CHANNELS = CHANS * BANDS
LEVELS = CHANNELS.bit_length() - 1
INNER = CHANS.bit_length() - 1
BLOCK = 16
AVG = 128
CODE_TOP = 32760.0
STEPS_PER_OCTAVE = 16.0
FLOOR = 2.0**-100
SAMPLES = 512
TILE = 2048
LAST = 256

STEPS = (
    (0, 0), (0, 2), (3, 0), (1, 2), (3, 3), (1, 1), (3, 1), (0, 3),
    (1, 3), (2, 1), (2, 3), (3, 2), (1, 0), (2, 2), (0, 1), (2, 0),
)
ARRIVE = (
    (0, 0), (3, 0), (1, 2), (3, 3), (1, 1), (2, 1), (0, 2), (1, 3),
    (3, 1), (2, 3), (1, 0), (3, 2), (2, 2), (0, 3), (0, 1), (2, 0),
)


def counts(level):
    return 1 if level == 0 else min(DELAYS, 2 ** (level + 1))


def kernel(v_ref, w_ref, order_hbm, table_hbm, out_ref, xbuf, wbuf, nbuf, acc, pws, norm, stage, send, recv, order,
           raw, cooked, table, state1, state2, state3, state4, state5, state6,
           x_send, x_recv, w_sem, o_sem, t_sem, ready, s_sem, r_sem):
    band = lax.axis_index("band")
    chan = lax.axis_index("chan")
    x, y = chan // SIDE, lax.rem(chan, SIDE)
    beams = w_ref.shape[3]

    def ahead(step):
        return lax.rem(x + step[0], SIDE) * SIDE + lax.rem(y + step[1], SIDE)

    def behind(step):
        return lax.rem(x + SIDE - step[0], SIDE) * SIDE + lax.rem(y + SIDE - step[1], SIDE)

    barrier = pltpu.get_barrier_semaphore()
    for step in STEPS[1:]:
        pl.semaphore_signal(barrier, inc=1, device_id={"band": band, "chan": ahead(step)}, device_id_type=MESH)
    for k in range(1, BANDS):
        pl.semaphore_signal(barrier, inc=1, device_id={"band": lax.rem(band + k, BANDS), "chan": chan}, device_id_type=MESH)

    pltpu.make_async_copy(v_ref.at[chan], xbuf.at[0], x_recv.at[0]).start()
    for k, step in enumerate(ARRIVE):
        rows = pl.ds(pl.multiple_of(behind(step) * 128, 128), 128)
        for part in range(2):
            pltpu.make_async_copy(w_ref.at[0, part, rows, :], wbuf.at[k, pl.ds(part * 128, 128), :], w_sem.at[k]).start()
    order_copy = pltpu.make_async_copy(order_hbm, order, o_sem)
    order_copy.start()
    raw_copy = pltpu.make_async_copy(table_hbm, raw, t_sem)
    raw_copy.start()

    def clear(i, carry):
        acc[pl.ds(pl.multiple_of(i * 8, 8), 8), :] = jnp.zeros((8, beams), jnp.float32)
        return carry

    lax.fori_loop(0, 2 * SAMPLES // 8, clear, 0)
    pl.semaphore_wait(barrier, CHANS - 1 + BANDS - 1)
    copies = []
    for step in STEPS[1:]:
        k = ARRIVE.index(step)
        peer = ahead(step)
        copy = pltpu.make_async_remote_copy(
            v_ref.at[peer], xbuf.at[k], x_send.at[k], x_recv.at[k],
            device_id={"band": band, "chan": peer}, device_id_type=MESH)
        copy.start()
        copies.append(copy)
    for step in STEPS[1:]:
        pl.semaphore_signal(ready, inc=1, device_id={"band": band, "chan": ahead(step)}, device_id_type=MESH)

    raw_copy.wait()
    node = lax.broadcasted_iota(jnp.int32, (DELAYS, CHANNELS - 1), 1)
    low_base = jnp.zeros((DELAYS, CHANNELS - 1), jnp.int32)
    high_base = low_base
    for level in range(1, LEVELS + 1):
        first = CHANNELS - (CHANNELS >> (level - 1))
        group = node - first
        if level <= INNER:
            group = lax.rem(group, CHANS >> level)
        low_base = jnp.where(node >= first, 2 * group * counts(level - 1), low_base)
        high_base = jnp.where(node >= first, (2 * group + 1) * counts(level - 1), high_base)
    cooked[0] = raw[0] + low_base
    cooked[1] = raw[1] + high_base
    cooked[2] = AVG - raw[2]

    def arrived(k):
        pltpu.make_async_copy(xbuf.at[k], xbuf.at[k], x_recv.at[k]).wait()
        pltpu.make_async_copy(wbuf.at[k], wbuf.at[k], w_sem.at[k]).wait()
        nbuf[...] = -xbuf[k, 1]

    def product(k, cols):
        top = jnp.concatenate([xbuf[k, 0], nbuf[...]], axis=1)
        low = jnp.concatenate([xbuf[k, 1], xbuf[k, 0]], axis=1)
        return jnp.dot(jnp.concatenate([top, low], axis=0), wbuf[k, :, cols], preferred_element_type=jnp.float32)

    def columns(n, width):
        return slice(n * width, (n + 1) * width)

    def block(k):
        arrived(k)

        for n in range(beams // TILE):
            cols = columns(n, TILE)
            acc[:, cols] += product(k, cols)

    table_copy = pltpu.make_async_copy(cooked, table, t_sem)
    table_copy.start()

    def later(k, carry):
        block(k)
        return carry

    lax.fori_loop(0, CHANS - 1, later, 0)
    arrived(CHANS - 1)

    def final(n):
        cols = columns(n, LAST)
        got = acc[:, cols] + product(CHANS - 1, cols)
        real, imag = got[:SAMPLES], got[SAMPLES:]
        power = real * real + imag * imag
        for half in range(LAST // 128):
            pw = pws.at[n % 2]
            pw[half] = power[:, half * 128 : (half + 1) * 128]
            total = pw[half, pl.ds(0, AVG, stride=4), :]
            for t in range(1, 4):
                total = total + pw[half, pl.ds(t, AVG, stride=4), :]
            mean4 = total * 0.25
            centered = mean4 - jnp.mean(mean4, axis=0, keepdims=True)
            centered = centered - jnp.mean(centered, axis=0, keepdims=True)
            spread = jnp.mean(centered * centered, axis=0, keepdims=True)
            inverse = 1.0 / jnp.sqrt(spread + 1e-05)
            top = jnp.max(jnp.abs(centered), axis=0, keepdims=True) * inverse
            code = jnp.ceil(jnp.log2(jnp.maximum(top, FLOOR)) * STEPS_PER_OCTAVE)
            grow = inverse * (CODE_TOP * jnp.exp2(code * (-1.0 / STEPS_PER_OCTAVE)))
            whole = jnp.round(centered * grow)
            times = lax.broadcasted_iota(jnp.int32, whole.shape, 0)
            scaled = jnp.where(times == AVG - 1, code, whole)
            at = n * LAST + half * 128
            norm[at : at + 128, :] = scaled.T

    for n in range(beams // LAST):
        final(n)
    for copy in copies:
        copy.wait_send()

    order_copy.wait()
    table_copy.wait()
    pl.semaphore_wait(ready, CHANS - 1)
    me = band * CHANS + chan

    def gather(slot, at, block):
        for i in range(BLOCK):
            stage[at, pl.ds(i, 1), :] = norm[pl.ds(order[block * BLOCK + i], 1), :]
        send[slot] = stage[at].astype(jnp.int32).astype(jnp.int16)

    to_chans = [ahead((rc // SIDE, rc % SIDE)) for rc in range(CHANS)]

    def send_some(j, carry):
        to_band = lax.rem(band + j, BANDS)
        for i in range(CHANS):
            slot = j * CHANS + i

            def one(slot=slot, i=i):
                gather(slot, i, to_band * CHANS + to_chans[i])
                pltpu.make_async_remote_copy(
                    send.at[slot], recv.at[me], s_sem, r_sem.at[band],
                    device_id={"band": to_band, "chan": to_chans[i]}, device_id_type=MESH).start()

            if i == 0:
                pl.when(j > 0)(one)
            else:
                one()
        return carry

    lax.fori_loop(0, BANDS, send_some, 0)
    gather(CHANNELS, 0, me)
    pltpu.make_async_copy(send.at[CHANNELS], recv.at[me], r_sem.at[band]).start()

    lanes = lax.broadcasted_iota(jnp.int32, (BLOCK, AVG), 1)

    def shifted(high, keep):
        return jnp.where(lanes < keep, pltpu.roll(high, keep, 1), 0.0)

    def merge(r, count, source, store):
        for d in range(count):
            low = source[table[0, d, r]]
            store(d, low + shifted(source[table[1, d, r]], table[2, d, r]))

    def decoded(channel):
        got = recv[channel].astype(jnp.int32).astype(jnp.float32)
        last = lanes == AVG - 1
        code = jnp.sum(jnp.where(last, got, 0.0), axis=1, keepdims=True)
        got = jnp.where(last, 0.0, got)
        got = got - jnp.where(last, jnp.sum(got, axis=1, keepdims=True), 0.0)
        return got * (jnp.exp2(code * (1.0 / STEPS_PER_OCTAVE)) * (1.0 / CODE_TOP))

    def one_band(k, carry):
        q = lax.rem(band + BANDS - k, BANDS)
        got = recv.at[pl.ds(q * CHANS, CHANS)]
        pltpu.make_async_copy(got, got, r_sem.at[q]).wait()
        for i in range(CHANS // 2):
            low = decoded(q * CHANS + 2 * i)
            high = decoded(q * CHANS + 2 * i + 1)
            for d in range(4):
                state1[i * 4 + d] = low + shifted(high, table[2, d, q * 8 + i])
        for i in range(4):
            def store2(d, merged, i=i):
                state2[i * 8 + d] = merged
            merge(64 + q * 4 + i, 8, state1, store2)
        for i in range(2):
            def store3(d, merged, i=i):
                state3[i * 16 + d] = merged
            merge(96 + q * 2 + i, 16, state2, store3)

        def store4(d, merged):
            state4[q * 32 + d] = merged
        merge(112 + q, 32, state3, store4)
        return carry

    lax.fori_loop(0, BANDS, one_band, 0)
    for g in range(4):
        def store5(d, merged, g=g):
            state5[g * DELAYS + d] = merged
        merge(120 + g, DELAYS, state4, store5)
    for g in range(2):
        def store6(d, merged, g=g):
            state6[g * DELAYS + d] = merged
        merge(124 + g, DELAYS, state5, store6)

    def store7(d, merged):
        out_ref[d] = merged * (1.0 / math.sqrt(CHANNELS))
    merge(126, DELAYS, state6, store7)
    others = pl.ds(0, CHANNELS - 1)
    pltpu.make_async_copy(send.at[others], send.at[others], s_sem).wait()


def body(voltages, weights, beam_order, delay_merge_tables):
    beams = weights.shape[3]
    any_space = pl.BlockSpec(memory_space=pl.ANY)
    few = (32, BLOCK, AVG)
    got = pl.pallas_call(
        kernel,
        out_shape=jax.ShapeDtypeStruct((DELAYS, BLOCK, AVG), jnp.float32),
        in_specs=[any_space] * 4,
        out_specs=pl.BlockSpec(memory_space=pltpu.VMEM),
        scratch_shapes=[
            pltpu.VMEM((CHANS, 2, SAMPLES, 128), jnp.bfloat16),
            pltpu.VMEM((CHANS, 256, beams), jnp.bfloat16),
            pltpu.VMEM((SAMPLES, 128), jnp.bfloat16),
            pltpu.VMEM((2 * SAMPLES, beams), jnp.float32),
            pltpu.VMEM((2, LAST // 128, SAMPLES, 128), jnp.float32),
            pltpu.VMEM((beams, AVG), jnp.float32),
            pltpu.VMEM((CHANS, BLOCK, AVG), jnp.float32),
            pltpu.VMEM((CHANNELS + 1, BLOCK, AVG), jnp.int16),
            pltpu.VMEM((CHANNELS, BLOCK, AVG), jnp.int16),
            pltpu.SMEM((beams,), jnp.int32),
            pltpu.VMEM((3, DELAYS, CHANNELS - 1), jnp.int32),
            pltpu.VMEM((3, DELAYS, CHANNELS - 1), jnp.int32),
            pltpu.SMEM((3, DELAYS, CHANNELS - 1), jnp.int32),
            pltpu.VMEM(few, jnp.float32),
            pltpu.VMEM(few, jnp.float32),
            pltpu.VMEM(few, jnp.float32),
            pltpu.VMEM((256, BLOCK, AVG), jnp.float32),
            pltpu.VMEM((256, BLOCK, AVG), jnp.float32),
            pltpu.VMEM((128, BLOCK, AVG), jnp.float32),
            pltpu.SemaphoreType.DMA((CHANS,)),
            pltpu.SemaphoreType.DMA((CHANS,)),
            pltpu.SemaphoreType.DMA((CHANS,)),
            pltpu.SemaphoreType.DMA,
            pltpu.SemaphoreType.DMA,
            pltpu.SemaphoreType.REGULAR,
            pltpu.SemaphoreType.DMA,
            pltpu.SemaphoreType.DMA((BANDS,)),
        ],
        compiler_params=pltpu.CompilerParams(
            collective_id=0, has_side_effects=True, vmem_limit_bytes=56 * 2**20),
    )(voltages, weights, beam_order, jnp.transpose(delay_merge_tables, (2, 1, 0)))
    return jnp.transpose(got, (1, 0, 2))


def solution(mesh):
    return jax.shard_map(
        body,
        mesh=mesh,
        in_specs=(P("band", None, None, "chan"), P(("band", "chan"), None, None, None), P(), P()),
        out_specs=P(("band", "chan"), None, None),
        check_vma=False,
    )
```

```python
import functools
import math

import jax
import jax.numpy as jnp
from jax import lax
from jax.experimental import pallas as pl
from jax.experimental.pallas import tpu as pltpu
from jax.sharding import PartitionSpec as P

MESH = pl.DeviceIdType.MESH
DELAYS = 64
SIDE = 4
CHANS = 16
BANDS = 8
CHANNELS = CHANS * BANDS
LEVELS = CHANNELS.bit_length() - 1
BLOCK = 16
AVG = 128
CODE_TOP = 32760.0
STEPS_PER_OCTAVE = 16.0
FLOOR = 2.0**-100
SAMPLES = 512
TILE = 2048
LAST = 256

STEPS = (
    (0, 0), (0, 2), (3, 0), (1, 2), (3, 3), (1, 1), (3, 1), (0, 3),
    (1, 3), (2, 1), (2, 3), (3, 2), (1, 0), (2, 2), (0, 1), (2, 0),
)
ARRIVE = (
    (0, 0), (3, 0), (1, 2), (3, 3), (1, 1), (2, 1), (0, 2), (1, 3),
    (3, 1), (2, 3), (1, 0), (3, 2), (2, 2), (0, 3), (0, 1), (2, 0),
)

FAR = (
    (2, 2), (2, 1), (1, 2), (2, 3), (3, 2), (1, 1), (3, 3), (1, 3),
    (3, 1), (2, 0), (0, 2), (1, 0), (0, 1), (3, 0), (0, 3), (0, 0),
)
SLOTS = tuple((i + 1) % CHANS for i in range(CHANS))


def counts(level):
    return 1 if level == 0 else min(DELAYS, 2 ** (level + 1))


def kernel(v_ref, w_ref, order_hbm, table_hbm, out_ref, xbuf, wbuf, nbuf, acc, pws, norm, stage, send, recv, order,
           raw, cooked, table, state1, state2, state3, state4, state5, state6,
           x_send, x_recv, w_sem, o_sem, t_sem, ready, s_sem, r_sem):
    band = lax.axis_index("band")
    chan = lax.axis_index("chan")
    x, y = chan // SIDE, lax.rem(chan, SIDE)
    beams = w_ref.shape[3]

    def ahead(step):
        return lax.rem(x + step[0], SIDE) * SIDE + lax.rem(y + step[1], SIDE)

    def behind(step):
        return lax.rem(x + SIDE - step[0], SIDE) * SIDE + lax.rem(y + SIDE - step[1], SIDE)

    barrier = pltpu.get_barrier_semaphore()
    for step in STEPS[1:]:
        pl.semaphore_signal(barrier, inc=1, device_id={"band": band, "chan": ahead(step)}, device_id_type=MESH)
    for k in range(1, BANDS):
        pl.semaphore_signal(barrier, inc=1, device_id={"band": lax.rem(band + k, BANDS), "chan": chan}, device_id_type=MESH)

    pltpu.make_async_copy(v_ref.at[chan], xbuf.at[0], x_recv.at[0]).start()
    for k, step in enumerate(ARRIVE):
        rows = pl.ds(pl.multiple_of(behind(step) * 128, 128), 128)
        for part in range(2):
            pltpu.make_async_copy(w_ref.at[0, part, rows, :], wbuf.at[k, pl.ds(part * 128, 128), :], w_sem.at[k]).start()
    order_copy = pltpu.make_async_copy(order_hbm, order, o_sem)
    order_copy.start()
    raw_copy = pltpu.make_async_copy(table_hbm, raw, t_sem)
    raw_copy.start()

    def clear(i, carry):
        acc[pl.ds(pl.multiple_of(i * 8, 8), 8), :] = jnp.zeros((8, beams), jnp.float32)
        return carry

    lax.fori_loop(0, 2 * SAMPLES // 8, clear, 0)
    pl.semaphore_wait(barrier, CHANS - 1 + BANDS - 1)
    copies = []
    for step in STEPS[1:]:
        k = ARRIVE.index(step)
        peer = ahead(step)
        copy = pltpu.make_async_remote_copy(
            v_ref.at[peer], xbuf.at[k], x_send.at[k], x_recv.at[k],
            device_id={"band": band, "chan": peer}, device_id_type=MESH)
        copy.start()
        copies.append(copy)
    for step in STEPS[1:]:
        pl.semaphore_signal(ready, inc=1, device_id={"band": band, "chan": ahead(step)}, device_id_type=MESH)

    raw_copy.wait()
    node = lax.broadcasted_iota(jnp.int32, (DELAYS, CHANNELS - 1), 1)
    low_base = jnp.zeros((DELAYS, CHANNELS - 1), jnp.int32)
    high_base = low_base
    for level in range(1, LEVELS + 1):
        first = CHANNELS - (CHANNELS >> (level - 1))
        group = node - first
        low_base = jnp.where(node >= first, 2 * group * counts(level - 1), low_base)
        high_base = jnp.where(node >= first, (2 * group + 1) * counts(level - 1), high_base)
    cooked[0] = raw[0] + low_base
    cooked[1] = raw[1] + high_base
    cooked[2] = AVG - raw[2]

    def arrived(k):
        pltpu.make_async_copy(xbuf.at[k], xbuf.at[k], x_recv.at[k]).wait()
        pltpu.make_async_copy(wbuf.at[k], wbuf.at[k], w_sem.at[k]).wait()
        nbuf[...] = -xbuf[k, 1]

    def product(k, cols):
        top = jnp.concatenate([xbuf[k, 0], nbuf[...]], axis=1)
        low = jnp.concatenate([xbuf[k, 1], xbuf[k, 0]], axis=1)
        return jnp.dot(jnp.concatenate([top, low], axis=0), wbuf[k, :, cols], preferred_element_type=jnp.float32)

    def columns(n, width):
        return slice(n * width, (n + 1) * width)

    def block(k):
        arrived(k)

        for n in range(beams // TILE):
            cols = columns(n, TILE)
            acc[:, cols] += product(k, cols)

    table_copy = pltpu.make_async_copy(cooked, table, t_sem)
    table_copy.start()

    def later(k, carry):
        block(k)
        return carry

    lax.fori_loop(0, CHANS - 1, later, 0)
    arrived(CHANS - 1)

    def final(n):
        cols = columns(n, LAST)
        pw = pws.at[n % 2]
        got = acc[:, cols] + product(CHANS - 1, cols)
        real, imag = got[:SAMPLES], got[SAMPLES:]
        power = real * real + imag * imag
        for half in range(LAST // 128):
            pw[half] = power[:, half * 128 : (half + 1) * 128]
        for half in range(LAST // 128):
            total = pw[half, pl.ds(0, AVG, stride=4), :]
            for t in range(1, 4):
                total = total + pw[half, pl.ds(t, AVG, stride=4), :]
            mean4 = total * 0.25
            centered = mean4 - jnp.mean(mean4, axis=0, keepdims=True)
            centered = centered - jnp.mean(centered, axis=0, keepdims=True)
            spread = jnp.mean(centered * centered, axis=0, keepdims=True)
            inverse = 1.0 / jnp.sqrt(spread + 1e-05)
            top = jnp.max(jnp.abs(centered), axis=0, keepdims=True) * inverse
            code = jnp.ceil(jnp.log2(jnp.maximum(top, FLOOR)) * STEPS_PER_OCTAVE)
            grow = inverse * (CODE_TOP * jnp.exp2(code * (-1.0 / STEPS_PER_OCTAVE)))
            whole = jnp.round(centered * grow)
            times = lax.broadcasted_iota(jnp.int32, whole.shape, 0)
            scaled = jnp.where(times == AVG - 1, code, whole)
            at = n * LAST + half * 128
            norm[at : at + 128, :] = scaled.T

    for n in range(beams // LAST):
        final(n)
    for copy in copies:
        copy.wait_send()

    order_copy.wait()
    table_copy.wait()
    pl.semaphore_wait(ready, CHANS - 1)
    me = band * CHANS + chan

    def gather(slot, at, block):
        for i in range(BLOCK):
            stage[at, pl.ds(i, 1), :] = norm[pl.ds(order[block * BLOCK + i], 1), :]
        send[slot] = stage[at].astype(jnp.int32).astype(jnp.int16)

    to_chans = [ahead(step) for step in FAR]

    def send_some(j, carry):
        to_band = lax.rem(band + j, BANDS)
        for i in range(CHANS):
            slot = j * CHANS + SLOTS[i]

            def one(slot=slot, i=i):
                gather(slot, i, to_band * CHANS + to_chans[i])
                pltpu.make_async_remote_copy(
                    send.at[slot], recv.at[me], s_sem, r_sem.at[band],
                    device_id={"band": to_band, "chan": to_chans[i]}, device_id_type=MESH).start()

            if FAR[i] == (0, 0):
                pl.when(j > 0)(one)
            else:
                one()
        return carry

    lax.fori_loop(0, BANDS, send_some, 0)
    gather(0, 0, me)
    pltpu.make_async_copy(send.at[0], recv.at[me], r_sem.at[band]).start()

    lanes = lax.broadcasted_iota(jnp.int32, (BLOCK, AVG), 1)

    def shifted(high, keep):
        return jnp.where(lanes < keep, pltpu.roll(high, keep, 1), 0.0)

    def decoded(channel):
        got = recv[channel].astype(jnp.int32).astype(jnp.float32)
        last = lanes == AVG - 1
        code = jnp.sum(jnp.where(last, got, 0.0), axis=1, keepdims=True)
        got = jnp.where(last, 0.0, got)
        got = got - jnp.where(last, jnp.sum(got, axis=1, keepdims=True), 0.0)
        return got * (jnp.exp2(code * (1.0 / STEPS_PER_OCTAVE)) * (1.0 / CODE_TOP))

    def one_band(j, carry):
        q = lax.rem(band + BANDS - j, BANDS)
        got = recv.at[pl.ds(q * CHANS, CHANS)]
        pltpu.make_async_copy(got, got, r_sem.at[q]).wait()
        for i in range(CHANS // 2):
            low = decoded(q * CHANS + 2 * i)
            high = decoded(q * CHANS + 2 * i + 1)
            for d in range(4):
                state1[q * 32 + i * 4 + d] = low + shifted(high, table[2, d, q * 8 + i])
        return carry

    lax.fori_loop(0, BANDS, one_band, 0)

    def merge(level, source, target):
        count = counts(level)
        for g in range(CHANNELS >> level):
            r = CHANNELS - (CHANNELS >> (level - 1)) + g
            for d in range(count):
                low = source[table[0, d, r]]
                merged = low + shifted(source[table[1, d, r]], table[2, d, r])
                if level == LEVELS:
                    target[pl.ds(d, BLOCK, stride=DELAYS), :] = merged
                else:
                    target[g * count + d] = merged

    states = (None, state1, state2, state3, state4, state5, state6, out_ref)
    for level in range(2, LEVELS + 1):
        merge(level, states[level - 1], states[level])
    others = pl.ds(1, CHANNELS - 1)
    pltpu.make_async_copy(send.at[others], send.at[others], s_sem).wait()


def body(voltages, weights, beam_order, delay_merge_tables):
    beams = weights.shape[3]
    any_space = pl.BlockSpec(memory_space=pl.ANY)
    whole = (256, BLOCK, AVG)
    got = pl.pallas_call(
        kernel,
        out_shape=jax.ShapeDtypeStruct((BLOCK * DELAYS, AVG), jnp.float32),
        in_specs=[any_space] * 4,
        out_specs=pl.BlockSpec(memory_space=pltpu.VMEM),
        scratch_shapes=[
            pltpu.VMEM((CHANS, 2, SAMPLES, 128), jnp.bfloat16),
            pltpu.VMEM((CHANS, 256, beams), jnp.bfloat16),
            pltpu.VMEM((SAMPLES, 128), jnp.bfloat16),
            pltpu.VMEM((2 * SAMPLES, beams), jnp.float32),
            pltpu.VMEM((2, LAST // 128, SAMPLES, 128), jnp.float32),
            pltpu.VMEM((beams, AVG), jnp.float32),
            pltpu.VMEM((CHANS, BLOCK, AVG), jnp.float32),
            pltpu.VMEM((CHANNELS, BLOCK, AVG), jnp.int16),
            pltpu.VMEM((CHANNELS, BLOCK, AVG), jnp.int16),
            pltpu.SMEM((beams,), jnp.int32),
            pltpu.VMEM((3, DELAYS, CHANNELS - 1), jnp.int32),
            pltpu.VMEM((3, DELAYS, CHANNELS - 1), jnp.int32),
            pltpu.SMEM((3, DELAYS, CHANNELS - 1), jnp.int32),
            pltpu.VMEM(whole, jnp.float32),
            pltpu.VMEM(whole, jnp.float32),
            pltpu.VMEM(whole, jnp.float32),
            pltpu.VMEM((256, BLOCK, AVG), jnp.float32),
            pltpu.VMEM((256, BLOCK, AVG), jnp.float32),
            pltpu.VMEM((128, BLOCK, AVG), jnp.float32),
            pltpu.SemaphoreType.DMA((CHANS,)),
            pltpu.SemaphoreType.DMA((CHANS,)),
            pltpu.SemaphoreType.DMA((CHANS,)),
            pltpu.SemaphoreType.DMA,
            pltpu.SemaphoreType.DMA,
            pltpu.SemaphoreType.REGULAR,
            pltpu.SemaphoreType.DMA,
            pltpu.SemaphoreType.DMA((BANDS,)),
        ],
        compiler_params=pltpu.CompilerParams(
            collective_id=0, has_side_effects=True, vmem_limit_bytes=52 * 2**20),
    )(voltages, weights, beam_order, jnp.transpose(delay_merge_tables, (2, 1, 0)))
    return got.reshape(BLOCK, DELAYS, AVG) * (1.0 / math.sqrt(CHANNELS))


def solution(mesh):
    return jax.shard_map(
        body,
        mesh=mesh,
        in_specs=(P("band", None, None, "chan"), P(("band", "chan"), None, None, None), P(), P()),
        out_specs=P(("band", "chan"), None, None),
        check_vma=False,
    )
```
